32 devices in a mesh: shot: 4 (over z), tile: 8 (over y, x, core).
Axes of the slice: x: 2, y: 2, z: 4, core: 2. Of those that a mesh axis runs over, the one named last changes fastest.
Arguments:
- traces: bfloat16 [2, 4, 1024, 2048], P(None, 'shot', 'tile'), may hold values from -6 to 6
- start: int32 [4, 8, 8], P('shot'), may hold values from 0 to 1536
- depth_index: int32 [4, 8, 8, 256], P('shot', 'tile'), may hold values from 0 to 510
- depth_frac: bfloat16 [4, 8, 8, 256], P('shot', 'tile'), may hold values from 0 to 1
- aperture: int32 [4, 8, 4], P('shot'), may hold values from -1 to 7, as said below
- amplitude: bfloat16 [4, 8, 8, 384, 128], P('shot', 'tile'), may hold values from -0.5 to 0.5
Outputs:
- migrated: float32 [3072, 256], P('tile', 'shot')
The draws below stay inside these ranges and needn't reach their ends.
Inputs may be any that keep to these rules, and one draw needn't show every extreme that they name: `aperture`: each list holds 1 to 4 block ids, ascending and consecutive, then -1 in the remaining slots; in every shot some tile's list is full.
All inputs are finite; a program needn't handle non-finite values.
Results may differ from the reference program's by a relative error of at most 0.0041.
Values may be sent and summed in bfloat16 or wider, within the bound.
No kernel may reach another device: no remote copies, remote signals or barrier semaphores. Data moves between devices by JAX's collectives and lax.ppermute only.
A program may use at most 64 MiB of HBM per device.

```python
import jax
import jax.numpy as jnp
from jax import lax

NT = 2048
RB = 128
TW = 512
C = 384
Z = 256
SHOTS = 4
RECV = 1024
A_MAX = 4
N_TILE = 8


def draw_start(key, part):
    values = jax.random.randint(jax.random.fold_in(key, 3), (SHOTS, N_TILE, N_TILE), 0, NT - TW + 1)
    values = values.at[:, 0, 0].set(0)
    values = values.at[:, N_TILE - 1, N_TILE - 1].set(NT - TW)
    return values.astype(jnp.int32)


def draw_depth_index(key, part):
    depth_pos = jnp.arange(Z)
    base_rows = depth_pos * (TW - 5) // max(Z - 1, 1)
    jitter = jax.random.randint(jax.random.fold_in(key, 5), (SHOTS, N_TILE, N_TILE, Z), 0, 4)
    values = base_rows + jitter
    values = values.at[..., 0].set(0)
    values = values.at[..., Z - 1].set(TW - 2)
    return values.astype(jnp.int32)


def draw_aperture(key, part):
    base_key = jax.random.fold_in(key, 11)
    first_key, second_key, third_key, fourth_key = jax.random.split(base_key, 4)
    upper = jax.random.randint(first_key, (SHOTS, N_TILE), 0, A_MAX)
    lower = jax.random.randint(second_key, (SHOTS, N_TILE), 0, A_MAX)
    counts = A_MAX - upper * lower // (2 * (A_MAX - 1))
    tile_pos = jnp.arange(N_TILE)[None, :]
    full_tile = jax.random.randint(third_key, (SHOTS, 1), 0, N_TILE)
    single_tile = (full_tile + 1) % N_TILE
    counts = jnp.where(tile_pos == full_tile, A_MAX, counts)
    counts = jnp.where(tile_pos == single_tile, 1, counts)
    spare = N_TILE - counts + 1
    first_block = jax.random.randint(fourth_key, (SHOTS, N_TILE), 0, N_TILE) % spare
    first_block = jnp.where(tile_pos == full_tile, N_TILE - A_MAX, first_block)
    slot_pos = jnp.arange(A_MAX)
    block_ids = first_block[:, :, None] + slot_pos[None, None, :]
    return jnp.where(slot_pos[None, None, :] < counts[:, :, None], block_ids, -1).astype(jnp.int32)


def block_levels(own_key, dims, pieces, smallest, high):
    def one(position, parts):
        draws = jax.random.uniform(jax.random.fold_in(jax.random.fold_in(own_key, 6), position), (parts,), jnp.float32, smallest / len(pieces), high / len(pieces))
        return jnp.repeat(jnp.exp(draws), dims[position] // parts).reshape((-1,) + (1,) * (len(dims) - position - 1))

    level = one(*pieces[0])
    for cut in pieces[1:]:
        level = level * one(*cut)
    return level


def centred(key, extent, scale, limit, cuts=(), kind=jnp.bfloat16):
    result = scale * jax.random.normal(key, extent, jnp.float32)
    if cuts:
        result = result * block_levels(key, extent, cuts, -0.22, 0.18)
    return jnp.clip(result, -limit, limit).astype(kind)


def setup_inputs(seed: int = 0) -> dict:
    key_of = jax.random.split(jax.random.key(seed), 7)
    return {
        "traces": centred(key_of[0], (2, SHOTS, RECV, NT), 1.0, 6.0, ((1, 4), (2, 8))),
        "start": draw_start(jax.random.fold_in(key_of[6], 71), 0),
        "depth_index": draw_depth_index(jax.random.fold_in(key_of[6], 71), 0),
        "depth_frac": jnp.clip(1.0 * jax.random.uniform(key_of[3], (SHOTS, N_TILE, N_TILE, Z), jnp.float32) ** block_levels(key_of[3], (SHOTS, N_TILE, N_TILE, Z), ((0, 4), (1, 8)), -0.2, 0.2), 0.0, 1.0).astype(jnp.bfloat16),
        "aperture": draw_aperture(jax.random.fold_in(key_of[6], 71), 0),
        "amplitude": centred(key_of[5], (SHOTS, N_TILE, N_TILE, C, RB), RB ** -0.5, 0.5, ((0, 4), (1, 8))),
    }


def to_depth(window, sample_rows, fraction):
    lower_sample = jnp.take(window, sample_rows, axis=2).astype(jnp.float32)
    upper_sample = jnp.take(window, sample_rows + 1, axis=2).astype(jnp.float32)
    weight = fraction.astype(jnp.float32)
    return ((1.0 - weight) * lower_sample + weight * upper_sample).astype(jnp.bfloat16)

def reference(traces, start, depth_index, depth_frac, aperture, amplitude):
    stack = jnp.zeros((N_TILE, C, Z), jnp.float32)
    coherent = jnp.zeros((2, N_TILE, C, Z), jnp.float32)
    for shot_pos in range(SHOTS):
        gather_now = traces[:, shot_pos]

        def one_tile(tile_pos):

            def one_slot(running, slot_pos):
                block_id = aperture[shot_pos, tile_pos, slot_pos]
                present = block_id >= 0
                block_safe = jnp.maximum(block_id, 0).astype(jnp.int32)
                first_sample = start[shot_pos, tile_pos, block_safe].astype(jnp.int32)
                window = lax.dynamic_slice(gather_now, (jnp.int32(0), (block_safe * RB).astype(jnp.int32), first_sample), (2, RB, TW))
                depth_traces = to_depth(window, depth_index[shot_pos, tile_pos, block_safe], depth_frac[shot_pos, tile_pos, block_safe])
                weights = amplitude[shot_pos, tile_pos, block_safe].astype(jnp.float32)
                contribution = jnp.einsum('cr,prz->pcz', weights, depth_traces.astype(jnp.float32))
                return (running + jnp.where(present, contribution, jnp.zeros_like(contribution)), None)
            partial_sum, unused = lax.scan(one_slot, jnp.zeros((2, C, Z), jnp.float32), jnp.arange(A_MAX))
            return partial_sum
        partial_value = lax.map(one_tile, jnp.arange(N_TILE))
        magnitude = jnp.sqrt(partial_value[:, 0] ** 2 + partial_value[:, 1] ** 2)
        inverse = 1.0 / jnp.maximum(magnitude, 1.0)
        stack = stack + partial_value[:, 0]
        coherent = coherent + jnp.stack([partial_value[:, 0] * inverse, partial_value[:, 1] * inverse])
    migrated = stack * (coherent[0] ** 2 + coherent[1] ** 2) / (SHOTS * SHOTS)
    return migrated.reshape(N_TILE * C, Z)
```

```python
import functools

import jax
import jax.numpy as jnp
from jax import lax
from jax.experimental import pallas as pl
from jax.experimental.pallas import tpu as pltpu
from jax.sharding import PartitionSpec as P

TW = 512
LANES = 128
SLAB = TW + LANES
NT_DIMS = (((1,), (1,)), ((), ()))


def partner(pos, step, count):
    if count & (count - 1) == 0:
        return pos ^ step
    return (pos + step) % count


def source_of(pos, step, count):
    if count & (count - 1) == 0:
        return pos ^ step
    return (pos - step + count) % count


def pairs(step, count):
    return [(pos, partner(pos, step, count)) for pos in range(count)]


def depth_kernel(tiles, start_ref, aperture_ref, rows_ref, frac_ref, traces_ref, *out_refs):
    me = lax.axis_index("tile")
    samples = traces_ref.shape[2]
    depth = rows_ref.shape[1]
    rows_columns = rows_ref[...].T
    frac_columns = frac_ref[...].T
    column = lax.broadcasted_iota(jnp.int32, rows_columns.shape, 1)
    lane = lax.broadcasted_iota(jnp.int32, (depth, SLAB), 1).astype(jnp.float32)
    for step in range(tiles):
        tile = partner(me, step, tiles)
        listed = aperture_ref[tile, 0] == me
        for slot in range(1, aperture_ref.shape[1]):
            listed = jnp.logical_or(listed, aperture_ref[tile, slot] == me)
        out_ref = out_refs[step]

        @pl.when(listed)
        def _():
            first = start_ref[tile, me]
            slab = jnp.minimum(first // LANES, (samples - SLAB) // LANES) * LANES
            slab = pl.multiple_of(slab, LANES)
            mine = column == tile
            row = jnp.sum(jnp.where(mine, rows_columns, 0.0), axis=1, keepdims=True)
            weight = jnp.sum(jnp.where(mine, frac_columns, 0.0), axis=1, keepdims=True)
            row = row + (first - slab).astype(jnp.float32)
            lower_hot = (lane == row).astype(jnp.bfloat16)
            upper_hot = (lane == row + 1.0).astype(jnp.bfloat16)
            window = jnp.concatenate(
                [traces_ref[0, :, pl.ds(slab, SLAB)], traces_ref[1, :, pl.ds(slab, SLAB)]], axis=0
            )
            lower = lax.dot_general(lower_hot, window, NT_DIMS, preferred_element_type=jnp.float32)
            upper = lax.dot_general(upper_hot, window, NT_DIMS, preferred_element_type=jnp.float32)
            out_ref[...] = ((1.0 - weight) * lower + weight * upper).astype(jnp.bfloat16)

        @pl.when(jnp.logical_not(listed))
        def _():
            out_ref[...] = jnp.zeros_like(out_ref)


def partial_kernel(tiles, shots, amplitude_ref, *refs):
    me = lax.axis_index("tile")
    my_shot = lax.axis_index("shot")
    depth_refs = refs[:tiles]
    own_ref, out_refs, total_ref = refs[tiles], refs[tiles + 1 : -1], refs[-1]
    receivers = amplitude_ref.shape[2]
    piece = own_ref.shape[1]
    group = 8
    for base in range(0, tiles, group):
        steps = range(base, min(base + group, tiles))
        weights = jnp.concatenate(
            [amplitude_ref[source_of(me, step, tiles)] for step in steps], axis=1
        )
        for part in range(2):
            traces = jnp.concatenate(
                [
                    depth_refs[step][:, part * receivers : (part + 1) * receivers]
                    for step in steps
                ],
                axis=1,
            )
            added = lax.dot_general(traces, weights, NT_DIMS, preferred_element_type=jnp.float32)
            if base:
                added = added + total_ref[part]
            total_ref[part] = added
    for part in range(2):
        own_ref[part] = total_ref[part, pl.ds(pl.multiple_of(my_shot * piece, piece), piece), :]
        for step in range(1, shots):
            target = partner(my_shot, step, shots)
            rows = pl.ds(pl.multiple_of(target * piece, piece), piece)
            out_refs[step - 1][part] = total_ref[part, rows, :].astype(jnp.bfloat16)


def image_kernel(shots, *refs):
    out_ref = refs[-1]
    stack = None
    for ref in refs[:shots]:
        real = ref[0].astype(jnp.float32)
        imag = ref[1].astype(jnp.float32)
        inverse = 1.0 / jnp.maximum(jnp.sqrt(real * real + imag * imag), 1.0)
        if stack is None:
            stack, first, second = real, real * inverse, imag * inverse
        else:
            stack = stack + real
            first = first + real * inverse
            second = second + imag * inverse
    out_ref[...] = stack * (first * first + second * second) / (shots * shots)


VMEM = pl.BlockSpec(memory_space=pltpu.VMEM)
SMEM = pl.BlockSpec(memory_space=pltpu.SMEM)


def local(traces, start, depth_index, depth_frac, aperture, amplitude):
    tiles = lax.axis_size("tile")
    shots = lax.axis_size("shot")
    parts, _, receivers, samples = traces.shape
    depth = depth_index.shape[3]
    columns = amplitude.shape[3]
    piece = depth // shots

    wanted = jnp.stack(
        [depth_index[0, 0].astype(jnp.float32), depth_frac[0, 0].astype(jnp.float32)], axis=1
    )
    wanted = lax.all_to_all(wanted, "tile", split_axis=0, concat_axis=0, tiled=True)

    block = jax.ShapeDtypeStruct((depth, parts * receivers), jnp.bfloat16)
    sent = pl.pallas_call(
        functools.partial(depth_kernel, tiles),
        out_shape=[block] * tiles,
        in_specs=[SMEM, SMEM, VMEM, VMEM, VMEM],
        out_specs=[VMEM] * tiles,
        compiler_params=pltpu.CompilerParams(vmem_limit_bytes=32 << 20),
    )(start[0], aperture[0], wanted[:, 0], wanted[:, 1], traces[:, 0])
    received = [sent[0]]
    for step in range(1, tiles):
        received.append(lax.ppermute(sent[step], "tile", pairs(step, tiles)))

    own = jax.ShapeDtypeStruct((parts, piece, columns), jnp.float32)
    other = jax.ShapeDtypeStruct((parts, piece, columns), jnp.bfloat16)
    pieces = pl.pallas_call(
        functools.partial(partial_kernel, tiles, shots),
        out_shape=[own] + [other] * (shots - 1),
        in_specs=[VMEM] * (1 + tiles),
        out_specs=[VMEM] * shots,
        scratch_shapes=[pltpu.VMEM((parts, depth, columns), jnp.float32)],
        compiler_params=pltpu.CompilerParams(vmem_limit_bytes=32 << 20),
    )(amplitude[0, 0], *received)
    summed = [pieces[0]]
    for step in range(1, shots):
        summed.append(lax.ppermute(pieces[step], "shot", pairs(step, shots)))

    image = pl.pallas_call(
        functools.partial(image_kernel, shots),
        out_shape=jax.ShapeDtypeStruct((piece, columns), jnp.float32),
        in_specs=[VMEM] * shots,
        out_specs=VMEM,
    )(*summed)
    return image.T


def solution(mesh):
    in_specs = (
        P(None, "shot", "tile", None),
        P("shot", None, None),
        P("shot", "tile", None, None),
        P("shot", "tile", None, None),
        P("shot", None, None),
        P("shot", "tile", None, None, None),
    )
    out_specs = P("tile", "shot")
    return jax.shard_map(local, mesh=mesh, in_specs=in_specs, out_specs=out_specs, check_vma=False)
```

```python
import functools

import jax
import jax.numpy as jnp
from jax import lax
from jax.experimental import pallas as pl
from jax.experimental.pallas import tpu as pltpu
from jax.sharding import PartitionSpec as P

TW = 512
LANES = 128
SLAB = TW + LANES
CHUNKS = 1
NT_DIMS = (((1,), (1,)), ((), ()))
VMEM = pl.BlockSpec(memory_space=pltpu.VMEM)
SMEM = pl.BlockSpec(memory_space=pltpu.SMEM)


def target_of(pos, step, count):
    if count & (count - 1) == 0:
        return pos ^ step
    return (pos + step) % count


def source_of(pos, step, count):
    if count & (count - 1) == 0:
        return pos ^ step
    return (pos - step + count) % count


def pairs(step, count):
    return [(pos, target_of(pos, step, count)) for pos in range(count)]


def chip_pairs(step, tiles):
    return [
        (pos, 2 * target_of(pos // 2, step, tiles // 2) + pos % 2) for pos in range(tiles)
    ]


def steps_of(count):
    return list(range(count - 1, 0, -1))


def wanted_kernel(tiles, index_ref, frac_ref, *out_refs):
    me = lax.axis_index("tile")
    rows = index_ref[...].astype(jnp.float32)
    weights = frac_ref[...].astype(jnp.float32)
    position = lax.broadcasted_iota(jnp.int32, rows.shape, 0)
    for step, out_ref in enumerate(out_refs):
        block = 2 * source_of(me // 2, step, tiles // 2) + me % 2 if step else me
        for other in range(2):
            mine = position == (block ^ other)
            out_ref[other : other + 1] = jnp.sum(
                jnp.where(mine, rows, 0.0), axis=0, keepdims=True
            )
            out_ref[2 + other : 3 + other] = jnp.sum(
                jnp.where(mine, weights, 0.0), axis=0, keepdims=True
            )


def depth_kernel(tiles, shots, chunks, steps, start_ref, aperture_ref, own_ref, other_ref, *refs):
    me = lax.axis_index("tile")
    wanted_refs, out_refs = refs[: len(steps)], refs[len(steps) :]
    samples = own_ref.shape[2]
    depth = wanted_refs[0].shape[1]
    piece = depth // shots
    span = piece // chunks
    lane = lax.broadcasted_iota(jnp.int32, (depth // chunks, SLAB), 1).astype(jnp.float32)
    for place, step in enumerate(steps):
        tile = 2 * target_of(me // 2, step, tiles // 2) + me % 2 if step else me
        columns = wanted_refs[place][...].T
        for other, traces_ref in enumerate((own_ref, other_ref)):
            block = me ^ other
            listed = aperture_ref[tile, 0] == block
            for slot in range(1, aperture_ref.shape[1]):
                listed = jnp.logical_or(listed, aperture_ref[tile, slot] == block)
            outs = out_refs[place * chunks : (place + 1) * chunks]

            @pl.when(listed)
            def _():
                first = start_ref[tile, block]
                slab = jnp.minimum(first // LANES, (samples - SLAB) // LANES) * LANES
                slab = pl.multiple_of(slab, LANES)
                window = jnp.concatenate(
                    [traces_ref[0, :, pl.ds(slab, SLAB)], traces_ref[1, :, pl.ds(slab, SLAB)]],
                    axis=0,
                )
                shift = (first - slab).astype(jnp.float32)
                for chunk in range(chunks):
                    mine = jnp.concatenate(
                        [
                            columns[shot * piece + chunk * span : shot * piece + (chunk + 1) * span]
                            for shot in range(shots)
                        ],
                        axis=0,
                    )
                    row = mine[:, other : other + 1] + shift
                    weight = mine[:, 2 + other : 3 + other]
                    lower_hot = (lane == row).astype(jnp.bfloat16)
                    upper_hot = (lane == row + 1.0).astype(jnp.bfloat16)
                    lower = lax.dot_general(
                        lower_hot, window, NT_DIMS, preferred_element_type=jnp.float32
                    )
                    upper = lax.dot_general(
                        upper_hot, window, NT_DIMS, preferred_element_type=jnp.float32
                    )
                    outs[chunk][other] = ((1.0 - weight) * lower + weight * upper).astype(
                        jnp.bfloat16
                    )

            @pl.when(jnp.logical_not(listed))
            def _():
                for out_ref in outs:
                    out_ref[other] = jnp.zeros(out_ref.shape[1:], out_ref.dtype)


def partial_kernel(tiles, shots, steps, amplitude_ref, *refs):
    me = lax.axis_index("tile")
    my_shot = lax.axis_index("shot")
    depth_refs = refs[: len(steps)]
    own_ref, out_refs, total_ref = refs[len(steps)], refs[len(steps) + 1 : -1], refs[-1]
    receivers = amplitude_ref.shape[2]
    span = own_ref.shape[1]
    group = 4
    for base in range(0, len(steps), group):
        places = range(base, min(base + group, len(steps)))
        weights = []
        for place in places:
            step = steps[place]
            block = 2 * source_of(me // 2, step, tiles // 2) + me % 2 if step else me
            weights += [amplitude_ref[block], amplitude_ref[block ^ 1]]
        weights = jnp.concatenate(weights, axis=1)
        for part in range(2):
            lanes = slice(part * receivers, (part + 1) * receivers)
            traces = jnp.concatenate(
                [depth_refs[place][other, :, lanes] for place in places for other in range(2)],
                axis=1,
            )
            added = lax.dot_general(traces, weights, NT_DIMS, preferred_element_type=jnp.float32)
            if base:
                added = added + total_ref[part]
            total_ref[part] = added
    for part in range(2):
        own_ref[part] = total_ref[part, pl.ds(pl.multiple_of(my_shot * span, span), span), :]
        for place, step in enumerate(steps_of(shots)):
            target = target_of(my_shot, step, shots)
            rows = pl.ds(pl.multiple_of(target * span, span), span)
            out_refs[place][part] = total_ref[part, rows, :].astype(jnp.bfloat16)


def image_kernel(shots, chunks, *refs):
    out_ref = refs[-1]
    for chunk in range(chunks):
        stack = None
        for ref in refs[chunk * shots : (chunk + 1) * shots]:
            real = ref[0].astype(jnp.float32)
            imag = ref[1].astype(jnp.float32)
            inverse = 1.0 / jnp.maximum(jnp.sqrt(real * real + imag * imag), 1.0)
            if stack is None:
                stack, first, second = real, real * inverse, imag * inverse
            else:
                stack = stack + real
                first = first + real * inverse
                second = second + imag * inverse
        span = stack.shape[0]
        out_ref[chunk * span : (chunk + 1) * span] = (
            stack * (first * first + second * second) / (shots * shots)
        )


def local(traces, start, depth_index, depth_frac, aperture, amplitude):
    tiles = lax.axis_size("tile")
    shots = lax.axis_size("shot")
    parts, _, receivers, samples = traces.shape
    depth = depth_index.shape[3]
    columns = amplitude.shape[3]
    piece = depth // shots
    chunks = CHUNKS if piece % (16 * CHUNKS) == 0 else 1
    span = piece // chunks
    away = steps_of(tiles // 2)
    params = pltpu.CompilerParams(vmem_limit_bytes=32 << 20)
    small = pltpu.CompilerParams(vmem_limit_bytes=8 << 20)

    own_traces = traces[:, 0]
    other_traces = lax.ppermute(own_traces, "tile", [(pos, pos ^ 1) for pos in range(tiles)])

    wanted = pl.pallas_call(
        functools.partial(wanted_kernel, tiles),
        out_shape=[jax.ShapeDtypeStruct((4, depth), jnp.float32)] * (tiles // 2),
        in_specs=[VMEM, VMEM],
        out_specs=[VMEM] * (tiles // 2),
        compiler_params=small,
    )(depth_index[0, 0], depth_frac[0, 0])
    asked = [lax.ppermute(wanted[step], "tile", chip_pairs(step, tiles)) for step in away]

    def depth_traces(steps, requests):
        block = jax.ShapeDtypeStruct((2, depth // chunks, parts * receivers), jnp.bfloat16)
        return pl.pallas_call(
            functools.partial(depth_kernel, tiles, shots, chunks, steps),
            out_shape=[block] * (len(steps) * chunks),
            in_specs=[SMEM, SMEM, VMEM, VMEM] + [VMEM] * len(steps),
            out_specs=[VMEM] * (len(steps) * chunks),
            compiler_params=params,
        )(start[0], aperture[0], own_traces, other_traces, *requests)

    kept = depth_traces([0], [wanted[0]])
    sent = depth_traces(away, asked)

    own = jax.ShapeDtypeStruct((parts, span, columns), jnp.float32)
    other = jax.ShapeDtypeStruct((parts, span, columns), jnp.bfloat16)
    received = [
        [
            lax.ppermute(sent[place * chunks + chunk], "tile", chip_pairs(step, tiles))
            for place, step in enumerate(away)
        ]
        for chunk in range(chunks)
    ]
    summed = []
    for chunk in range(chunks):
        pieces = pl.pallas_call(
            functools.partial(partial_kernel, tiles, shots, [0] + away),
            out_shape=[own] + [other] * (shots - 1),
            in_specs=[VMEM] * (1 + tiles // 2),
            out_specs=[VMEM] * shots,
            scratch_shapes=[pltpu.VMEM((parts, depth // chunks, columns), jnp.float32)],
            compiler_params=params,
        )(amplitude[0, 0], kept[chunk], *received[chunk])
        summed.append(pieces[0])
        for place, step in enumerate(steps_of(shots)):
            summed.append(lax.ppermute(pieces[1 + place], "shot", pairs(step, shots)))

    image = pl.pallas_call(
        functools.partial(image_kernel, shots, chunks),
        out_shape=jax.ShapeDtypeStruct((piece, columns), jnp.float32),
        in_specs=[VMEM] * (shots * chunks),
        out_specs=VMEM,
        compiler_params=small,
    )(*summed)
    return image.T


def solution(mesh):
    in_specs = (
        P(None, "shot", "tile", None),
        P("shot", None, None),
        P("shot", "tile", None, None),
        P("shot", "tile", None, None),
        P("shot", None, None),
        P("shot", "tile", None, None, None),
    )
    out_specs = P("tile", "shot")
    return jax.shard_map(local, mesh=mesh, in_specs=in_specs, out_specs=out_specs, check_vma=False)
```

```python
import functools

import jax
import jax.numpy as jnp
from jax import lax
from jax.experimental import pallas as pl
from jax.experimental.pallas import tpu as pltpu
from jax.sharding import PartitionSpec as P

TW = 512
LANES = 128
SLAB = TW + LANES
NT_DIMS = (((1,), (1,)), ((), ()))
VMEM = pl.BlockSpec(memory_space=pltpu.VMEM)
HBM = pl.BlockSpec(memory_space=pltpu.HBM)


def target_of(pos, step, count):
    if count & (count - 1) == 0:
        return pos ^ step
    return (pos + step) % count


def source_of(pos, step, count):
    if count & (count - 1) == 0:
        return pos ^ step
    return (pos - step + count) % count


def pairs(step, count):
    return [(pos, target_of(pos, step, count)) for pos in range(count)]


def chip_pairs(step, tiles):
    return [
        (pos, 2 * target_of(pos // 2, step, tiles // 2) + pos % 2) for pos in range(tiles)
    ]


def steps_of(count):
    return list(range(count - 1, 0, -1))


def far_first(count):
    return sorted(range(1, count), key=lambda step: (step.bit_count(), -step))


def chip_of(step, tiles):
    me = lax.axis_index("tile")
    if step == 0:
        return me, me
    chips = tiles // 2
    served = 2 * target_of(me // 2, step, chips) + me % 2
    return served, 2 * source_of(me // 2, step, chips) + me % 2


def wanted_kernel(tiles, index_hbm, frac_hbm, start_hbm, aperture_hbm, traces_hbm, *refs):
    traces_ref, codes_ref, *out_refs, index_ref, frac_ref, start_ref, aperture_ref, sems = refs
    copies = [
        pltpu.make_async_copy(source, target, sems.at[place])
        for place, (source, target) in enumerate(
            [
                (index_hbm, index_ref),
                (frac_hbm, frac_ref),
                (start_hbm, start_ref),
                (aperture_hbm, aperture_ref),
                (traces_hbm, traces_ref),
            ]
        )
    ]
    for copy in copies:
        copy.start()
    for copy in copies[:4]:
        copy.wait()
    me = lax.axis_index("tile")
    rows = index_ref[...].astype(jnp.float32)
    weights = frac_ref[...].astype(jnp.float32)
    starts = start_ref[...]
    slots = aperture_ref[...]
    position = lax.broadcasted_iota(jnp.int32, rows.shape, 0)
    start_tile = lax.broadcasted_iota(jnp.int32, starts.shape, 0)
    start_block = lax.broadcasted_iota(jnp.int32, starts.shape, 1)
    slot_tile = lax.broadcasted_iota(jnp.int32, slots.shape, 1)
    for step, out_ref in enumerate(out_refs):
        tile, block = chip_of(step, tiles)
        for other in range(2):
            mine = position == (block ^ other)
            out_ref[other : other + 1] = jnp.sum(
                jnp.where(mine, rows, 0.0), axis=0, keepdims=True
            )
            out_ref[2 + other : 3 + other] = jnp.sum(
                jnp.where(mine, weights, 0.0), axis=0, keepdims=True
            )
            here = jnp.logical_and(start_tile == tile, start_block == (me ^ other))
            first = jnp.where(here, starts, 0).astype(jnp.float32)
            first = jnp.sum(jnp.sum(first, axis=1, keepdims=True), axis=0, keepdims=True)
            hits = jnp.logical_and(slot_tile == tile, slots == (me ^ other))
            hits = jnp.where(hits, 1.0, 0.0)
            hits = jnp.max(jnp.max(hits, axis=1, keepdims=True), axis=0, keepdims=True)
            code = jnp.where(hits > 0.0, first, -1.0).astype(jnp.int32)
            place = 2 * step + other
            codes_ref[place : place + 1] = jnp.broadcast_to(code, (1, codes_ref.shape[1]))
    copies[4].wait()


def interpolate(columns, other, shift, window):
    row = columns[:, other : other + 1] + shift
    weight = columns[:, 2 + other : 3 + other]
    depth = row.shape[0]
    lane = lax.broadcasted_iota(jnp.int32, (depth, window.shape[1]), 1).astype(jnp.float32)
    hot = jnp.concatenate(
        [(lane == row).astype(jnp.bfloat16), (lane == row + 1.0).astype(jnp.bfloat16)], axis=0
    )
    both = lax.dot_general(hot, window, NT_DIMS, preferred_element_type=jnp.float32)
    return ((1.0 - weight) * both[:depth] + weight * both[depth:]).astype(jnp.bfloat16)


def depth_kernel(step, codes_ref, own_ref, other_ref, wanted_ref, out_ref):
    last = own_ref.shape[2] // LANES - SLAB // LANES
    columns = wanted_ref[...].T
    for other, traces_ref in enumerate((own_ref, other_ref)):
        first = codes_ref[2 * step + other, 0]

        @pl.when(first >= 0)
        def _():
            slab = pl.multiple_of(jnp.minimum(first // LANES, last) * LANES, LANES)
            window = jnp.concatenate(
                [traces_ref[0, :, pl.ds(slab, SLAB)], traces_ref[1, :, pl.ds(slab, SLAB)]], axis=0
            )
            shift = (first - slab).astype(jnp.float32)
            out_ref[other] = interpolate(columns, other, shift, window)

        @pl.when(first < 0)
        def _():
            out_ref[other] = jnp.zeros(out_ref.shape[1:], out_ref.dtype)


def partial_kernel(tiles, shots, steps, amplitude_ref, *refs):
    my_shot = lax.axis_index("shot")
    depth_refs = refs[: len(steps)]
    own_ref, out_refs, total_ref = refs[len(steps)], refs[len(steps) + 1 : -1], refs[-1]
    receivers = amplitude_ref.shape[2]
    span = own_ref.shape[1]
    group = 4
    for base in range(0, len(steps), group):
        places = range(base, min(base + group, len(steps)))
        weights = []
        for place in places:
            _, block = chip_of(steps[place], tiles)
            weights += [amplitude_ref[block], amplitude_ref[block ^ 1]]
        weights = jnp.concatenate(weights, axis=1)
        for part in range(2):
            lanes = slice(part * receivers, (part + 1) * receivers)
            traces = jnp.concatenate(
                [depth_refs[place][other, :, lanes] for place in places for other in range(2)],
                axis=1,
            )
            added = lax.dot_general(traces, weights, NT_DIMS, preferred_element_type=jnp.float32)
            if base:
                added = added + total_ref[part]
            total_ref[part] = added
    for part in range(2):
        own_ref[part] = total_ref[part, pl.ds(pl.multiple_of(my_shot * span, span), span), :]
        for place, step in enumerate(steps_of(shots)):
            target = target_of(my_shot, step, shots)
            rows = pl.ds(pl.multiple_of(target * span, span), span)
            out_refs[place][part] = total_ref[part, rows, :].astype(jnp.bfloat16)


def image_kernel(shots, *refs):
    out_ref = refs[-1]
    stack = None
    for ref in refs[:shots]:
        real = ref[0].astype(jnp.float32)
        imag = ref[1].astype(jnp.float32)
        inverse = 1.0 / jnp.maximum(jnp.sqrt(real * real + imag * imag), 1.0)
        if stack is None:
            stack, first, second = real, real * inverse, imag * inverse
        else:
            stack = stack + real
            first = first + real * inverse
            second = second + imag * inverse
    out_ref[...] = stack * (first * first + second * second) / (shots * shots)


def local(traces, start, depth_index, depth_frac, aperture, amplitude):
    tiles = lax.axis_size("tile")
    shots = lax.axis_size("shot")
    parts, _, receivers, samples = traces.shape
    depth = depth_index.shape[3]
    columns = amplitude.shape[3]
    piece = depth // shots
    chips = tiles // 2
    away = far_first(chips)
    params = pltpu.CompilerParams(vmem_limit_bytes=32 << 20)
    small = pltpu.CompilerParams(vmem_limit_bytes=8 << 20)

    other_traces = lax.ppermute(traces[:, 0], "tile", [(pos, pos ^ 1) for pos in range(tiles)])

    inputs = [depth_index[0, 0], depth_frac[0, 0], start[0], aperture[0].T, traces[:, 0]]
    own_traces, codes, *wanted = pl.pallas_call(
        functools.partial(wanted_kernel, tiles),
        out_shape=[
            jax.ShapeDtypeStruct((parts, receivers, samples), traces.dtype),
            jax.ShapeDtypeStruct((tiles, LANES), jnp.int32),
        ]
        + [jax.ShapeDtypeStruct((4, depth), jnp.float32)] * chips,
        in_specs=[HBM] * len(inputs),
        out_specs=[VMEM] * (2 + chips),
        scratch_shapes=[pltpu.VMEM(value.shape, value.dtype) for value in inputs[:-1]]
        + [pltpu.SemaphoreType.DMA((len(inputs),))],
        compiler_params=params,
    )(*[pltpu.with_memory_space_constraint(value, pltpu.HBM) for value in inputs])
    asked = {
        step: lax.ppermute(wanted[step], "tile", chip_pairs(step, tiles))
        for step in away
    }

    def depth_traces(step, request):
        return pl.pallas_call(
            functools.partial(depth_kernel, step),
            out_shape=jax.ShapeDtypeStruct((2, depth, parts * receivers), jnp.bfloat16),
            in_specs=[VMEM] * 4,
            out_specs=VMEM,
            compiler_params=params,
            cost_estimate=pl.CostEstimate(
                flops=8 * depth * SLAB * parts * receivers,
                bytes_accessed=8 * parts * receivers * (samples + depth),
                transcendentals=0,
            ),
        )(codes, own_traces, other_traces, request)

    kept = depth_traces(0, wanted[0])
    received = [kept]
    for step in away:
        request = asked[step]
        sent = depth_traces(step, request)
        received.append(lax.ppermute(sent, "tile", chip_pairs(step, tiles)))

    own = jax.ShapeDtypeStruct((parts, piece, columns), jnp.float32)
    other = jax.ShapeDtypeStruct((parts, piece, columns), jnp.bfloat16)
    pieces = pl.pallas_call(
        functools.partial(partial_kernel, tiles, shots, [0] + away),
        out_shape=[own] + [other] * (shots - 1),
        in_specs=[VMEM] * (1 + chips),
        out_specs=[VMEM] * shots,
        scratch_shapes=[pltpu.VMEM((parts, depth, columns), jnp.float32)],
        compiler_params=params,
    )(amplitude[0, 0], *received)
    summed = [pieces[0]]
    for place, step in enumerate(steps_of(shots)):
        summed.append(lax.ppermute(pieces[1 + place], "shot", pairs(step, shots)))

    image = pl.pallas_call(
        functools.partial(image_kernel, shots),
        out_shape=jax.ShapeDtypeStruct((piece, columns), jnp.float32),
        in_specs=[VMEM] * shots,
        out_specs=VMEM,
        compiler_params=small,
    )(*summed)
    return image.T


def solution(mesh):
    in_specs = (
        P(None, "shot", "tile", None),
        P("shot", None, None),
        P("shot", "tile", None, None),
        P("shot", "tile", None, None),
        P("shot", None, None),
        P("shot", "tile", None, None, None),
    )
    out_specs = P("tile", "shot")
    return jax.shard_map(local, mesh=mesh, in_specs=in_specs, out_specs=out_specs, check_vma=False)
```

```python
import functools

import jax
import jax.numpy as jnp
from jax import lax
from jax.experimental import pallas as pl
from jax.experimental.pallas import tpu as pltpu
from jax.sharding import PartitionSpec as P

TW = 512
LANES = 128
SLAB = TW + LANES
NT_DIMS = (((1,), (1,)), ((), ()))
VMEM = pl.BlockSpec(memory_space=pltpu.VMEM)
HBM = pl.BlockSpec(memory_space=pltpu.HBM)


def target_of(pos, step, count):
    if count & (count - 1) == 0:
        return pos ^ step
    return (pos + step) % count


def source_of(pos, step, count):
    if count & (count - 1) == 0:
        return pos ^ step
    return (pos - step + count) % count


def pairs(step, count):
    return [(pos, target_of(pos, step, count)) for pos in range(count)]


def chip_pairs(step, tiles):
    return [
        (pos, 2 * target_of(pos // 2, step, tiles // 2) + pos % 2) for pos in range(tiles)
    ]


def steps_of(count):
    return list(range(count - 1, 0, -1))


def far_first(count):
    return sorted(range(1, count), key=lambda step: (step.bit_count(), -step))


def chip_of(step, tiles):
    me = lax.axis_index("tile")
    if step == 0:
        return me, me
    chips = tiles // 2
    served = 2 * target_of(me // 2, step, chips) + me % 2
    return served, 2 * source_of(me // 2, step, chips) + me % 2


def wanted_kernel(tiles, index_hbm, frac_hbm, start_hbm, aperture_hbm, traces_hbm, *refs):
    traces_ref, codes_ref, *out_refs, index_ref, frac_ref, start_ref, aperture_ref, sems = refs
    copies = [
        pltpu.make_async_copy(source, target, sems.at[place])
        for place, (source, target) in enumerate(
            [
                (index_hbm, index_ref),
                (frac_hbm, frac_ref),
                (start_hbm, start_ref),
                (aperture_hbm, aperture_ref),
                (traces_hbm, traces_ref),
            ]
        )
    ]
    for copy in copies:
        copy.start()
    for copy in copies[:4]:
        copy.wait()
    me = lax.axis_index("tile")
    rows = index_ref[...].astype(jnp.float32)
    weights = frac_ref[...].astype(jnp.float32)
    starts = start_ref[...]
    slots = aperture_ref[...]
    position = lax.broadcasted_iota(jnp.int32, rows.shape, 0)
    start_tile = lax.broadcasted_iota(jnp.int32, starts.shape, 0)
    start_block = lax.broadcasted_iota(jnp.int32, starts.shape, 1)
    slot_tile = lax.broadcasted_iota(jnp.int32, slots.shape, 1)
    for step, out_ref in enumerate(out_refs):
        tile, block = chip_of(step, tiles)
        for other in range(2):
            mine = position == (block ^ other)
            out_ref[other : other + 1] = jnp.sum(
                jnp.where(mine, rows, 0.0), axis=0, keepdims=True
            )
            out_ref[2 + other : 3 + other] = jnp.sum(
                jnp.where(mine, weights, 0.0), axis=0, keepdims=True
            )
            here = jnp.logical_and(start_tile == tile, start_block == (me ^ other))
            first = jnp.where(here, starts, 0).astype(jnp.float32)
            first = jnp.sum(jnp.sum(first, axis=1, keepdims=True), axis=0, keepdims=True)
            hits = jnp.logical_and(slot_tile == tile, slots == (me ^ other))
            hits = jnp.where(hits, 1.0, 0.0)
            hits = jnp.max(jnp.max(hits, axis=1, keepdims=True), axis=0, keepdims=True)
            code = jnp.where(hits > 0.0, first, -1.0).astype(jnp.int32)
            place = 2 * step + other
            codes_ref[place : place + 1] = jnp.broadcast_to(code, (1, codes_ref.shape[1]))
    copies[4].wait()


def interpolate(columns, other, shift, window):
    row = columns[:, other : other + 1] + shift
    weight = columns[:, 2 + other : 3 + other]
    depth = row.shape[0]
    lane = lax.broadcasted_iota(jnp.int32, (depth, window.shape[1]), 1).astype(jnp.float32)
    hot = jnp.concatenate(
        [(lane == row).astype(jnp.bfloat16), (lane == row + 1.0).astype(jnp.bfloat16)], axis=0
    )
    both = lax.dot_general(hot, window, NT_DIMS, preferred_element_type=jnp.float32)
    return ((1.0 - weight) * both[:depth] + weight * both[depth:]).astype(jnp.bfloat16)


def depth_kernel(step, codes_ref, own_ref, other_ref, wanted_ref, out_ref):
    last = own_ref.shape[2] // LANES - SLAB // LANES
    columns = wanted_ref[...].T
    for other, traces_ref in enumerate((own_ref, other_ref)):
        first = codes_ref[2 * step + other, 0]

        @pl.when(first >= 0)
        def _():
            slab = pl.multiple_of(jnp.minimum(first // LANES, last) * LANES, LANES)
            window = jnp.concatenate(
                [traces_ref[0, :, pl.ds(slab, SLAB)], traces_ref[1, :, pl.ds(slab, SLAB)]], axis=0
            )
            shift = (first - slab).astype(jnp.float32)
            out_ref[other] = interpolate(columns, other, shift, window)

        @pl.when(first < 0)
        def _():
            out_ref[other] = jnp.zeros(out_ref.shape[1:], out_ref.dtype)


def add_chips(tiles, steps, amplitude_ref, depth_refs, total_ref, fresh):
    receivers = amplitude_ref.shape[2]
    group = 4
    for base in range(0, len(steps), group):
        places = range(base, min(base + group, len(steps)))
        weights = []
        for place in places:
            _, block = chip_of(steps[place], tiles)
            weights += [amplitude_ref[block], amplitude_ref[block ^ 1]]
        weights = jnp.concatenate(weights, axis=1)
        for part in range(2):
            lanes = slice(part * receivers, (part + 1) * receivers)
            traces = jnp.concatenate(
                [depth_refs[place][other, :, lanes] for place in places for other in range(2)],
                axis=1,
            )
            added = lax.dot_general(traces, weights, NT_DIMS, preferred_element_type=jnp.float32)
            if base or not fresh:
                added = added + total_ref[part]
            total_ref[part] = added


def gather_kernel(tiles, steps, amplitude_ref, *refs):
    add_chips(tiles, steps, amplitude_ref, refs[:-1], refs[-1], True)


def partial_kernel(tiles, shots, steps, amplitude_ref, before_ref, *refs):
    my_shot = lax.axis_index("shot")
    depth_refs = refs[: len(steps)]
    own_ref, out_refs, total_ref = refs[len(steps)], refs[len(steps) + 1 : -1], refs[-1]
    span = own_ref.shape[1]
    total_ref[...] = before_ref[...]
    add_chips(tiles, steps, amplitude_ref, depth_refs, total_ref, False)
    for part in range(2):
        own_ref[part] = total_ref[part, pl.ds(pl.multiple_of(my_shot * span, span), span), :]
        for place, step in enumerate(steps_of(shots)):
            target = target_of(my_shot, step, shots)
            rows = pl.ds(pl.multiple_of(target * span, span), span)
            out_refs[place][part] = total_ref[part, rows, :].astype(jnp.bfloat16)


def add_shots(refs, sums):
    stack, first, second = sums
    for ref in refs:
        real = ref[0].astype(jnp.float32)
        imag = ref[1].astype(jnp.float32)
        inverse = 1.0 / jnp.maximum(jnp.sqrt(real * real + imag * imag), 1.0)
        stack, first, second = stack + real, first + real * inverse, second + imag * inverse
    return stack, first, second


def early_kernel(*refs):
    zero = jnp.zeros(refs[0].shape[1:], jnp.float32)
    sums = add_shots(refs[:-1], (zero, zero, zero))
    for place, value in enumerate(sums):
        refs[-1][place] = value


def image_kernel(shots, sums_ref, *refs):
    stack, first, second = add_shots(refs[:-1], (sums_ref[0], sums_ref[1], sums_ref[2]))
    refs[-1][...] = stack * (first * first + second * second) / (shots * shots)


def local(traces, start, depth_index, depth_frac, aperture, amplitude):
    tiles = lax.axis_size("tile")
    shots = lax.axis_size("shot")
    parts, _, receivers, samples = traces.shape
    depth = depth_index.shape[3]
    columns = amplitude.shape[3]
    piece = depth // shots
    chips = tiles // 2
    away = far_first(chips)
    params = pltpu.CompilerParams(vmem_limit_bytes=32 << 20)
    small = pltpu.CompilerParams(vmem_limit_bytes=8 << 20)

    other_traces = lax.ppermute(traces[:, 0], "tile", [(pos, pos ^ 1) for pos in range(tiles)])

    inputs = [depth_index[0, 0], depth_frac[0, 0], start[0], aperture[0].T, traces[:, 0]]
    own_traces, codes, *wanted = pl.pallas_call(
        functools.partial(wanted_kernel, tiles),
        out_shape=[
            jax.ShapeDtypeStruct((parts, receivers, samples), traces.dtype),
            jax.ShapeDtypeStruct((tiles, LANES), jnp.int32),
        ]
        + [jax.ShapeDtypeStruct((4, depth), jnp.float32)] * chips,
        in_specs=[HBM] * len(inputs),
        out_specs=[VMEM] * (2 + chips),
        scratch_shapes=[pltpu.VMEM(value.shape, value.dtype) for value in inputs[:-1]]
        + [pltpu.SemaphoreType.DMA((len(inputs),))],
        compiler_params=params,
    )(*[pltpu.with_memory_space_constraint(value, pltpu.HBM) for value in inputs])
    asked = {
        step: lax.ppermute(wanted[step], "tile", chip_pairs(step, tiles))
        for step in away
    }

    def depth_traces(step, request):
        return pl.pallas_call(
            functools.partial(depth_kernel, step),
            out_shape=jax.ShapeDtypeStruct((2, depth, parts * receivers), jnp.bfloat16),
            in_specs=[VMEM] * 4,
            out_specs=VMEM,
            compiler_params=params,
            cost_estimate=pl.CostEstimate(
                flops=8 * depth * SLAB * parts * receivers,
                bytes_accessed=8 * parts * receivers * (samples + depth),
                transcendentals=0,
            ),
        )(codes, own_traces, other_traces, request)

    kept = depth_traces(0, wanted[0])
    received = [kept]
    for step in away:
        request = asked[step]
        sent = depth_traces(step, request)
        received.append(lax.ppermute(sent, "tile", chip_pairs(step, tiles)))

    own = jax.ShapeDtypeStruct((parts, piece, columns), jnp.float32)
    other = jax.ShapeDtypeStruct((parts, piece, columns), jnp.bfloat16)
    steps = [0] + away
    total = jax.ShapeDtypeStruct((parts, depth, columns), jnp.float32)
    before = pl.pallas_call(
        functools.partial(gather_kernel, tiles, steps[:-1]),
        out_shape=total,
        in_specs=[VMEM] * chips,
        out_specs=VMEM,
        compiler_params=params,
    )(amplitude[0, 0], *received[:-1])
    pieces = pl.pallas_call(
        functools.partial(partial_kernel, tiles, shots, steps[-1:]),
        out_shape=[own] + [other] * (shots - 1),
        in_specs=[VMEM] * 3,
        out_specs=[VMEM] * shots,
        scratch_shapes=[pltpu.VMEM(total.shape, total.dtype)],
        compiler_params=params,
    )(amplitude[0, 0], before, received[-1])
    summed = [pieces[0]]
    for place, step in enumerate(steps_of(shots)):
        summed.append(lax.ppermute(pieces[1 + place], "shot", pairs(step, shots)))

    early = 2
    sums = pl.pallas_call(
        early_kernel,
        out_shape=jax.ShapeDtypeStruct((3, piece, columns), jnp.float32),
        in_specs=[VMEM] * early,
        out_specs=VMEM,
        compiler_params=params,
    )(*summed[:early])
    image = pl.pallas_call(
        functools.partial(image_kernel, shots),
        out_shape=jax.ShapeDtypeStruct((piece, columns), jnp.float32),
        in_specs=[VMEM] * (1 + shots - early),
        out_specs=VMEM,
        compiler_params=small,
    )(sums, *summed[early:])
    return image.T


def solution(mesh):
    in_specs = (
        P(None, "shot", "tile", None),
        P("shot", None, None),
        P("shot", "tile", None, None),
        P("shot", "tile", None, None),
        P("shot", None, None),
        P("shot", "tile", None, None, None),
    )
    out_specs = P("tile", "shot")
    return jax.shard_map(local, mesh=mesh, in_specs=in_specs, out_specs=out_specs, check_vma=False)
```

```python
import functools

import jax
import jax.numpy as jnp
from jax import lax
from jax.experimental import pallas as pl
from jax.experimental.pallas import tpu as pltpu
from jax.sharding import PartitionSpec as P

TW = 512
LANES = 128
SLAB = TW + LANES
NT_DIMS = (((1,), (1,)), ((), ()))
VMEM = pl.BlockSpec(memory_space=pltpu.VMEM)
HBM = pl.BlockSpec(memory_space=pltpu.HBM)


def target_of(pos, step, count):
    if count & (count - 1) == 0:
        return pos ^ step
    return (pos + step) % count


def source_of(pos, step, count):
    if count & (count - 1) == 0:
        return pos ^ step
    return (pos - step + count) % count


def pairs(step, count):
    return [(pos, target_of(pos, step, count)) for pos in range(count)]


def chip_pairs(step, tiles):
    return [
        (pos, 2 * target_of(pos // 2, step, tiles // 2) + pos % 2) for pos in range(tiles)
    ]


def steps_of(count):
    return list(range(count // 2, count)) + list(range(1, count // 2))


def near_first(count):
    return sorted(range(1, count), key=lambda step: (step.bit_count(), step))


def chip_of(step, tiles):
    me = lax.axis_index("tile")
    if step == 0:
        return me, me
    chips = tiles // 2
    served = 2 * target_of(me // 2, step, chips) + me % 2
    return served, 2 * source_of(me // 2, step, chips) + me % 2


def wanted_kernel(tiles, index_hbm, frac_hbm, start_hbm, aperture_hbm, traces_hbm, *refs):
    traces_ref, codes_ref, *out_refs, index_ref, frac_ref, start_ref, aperture_ref, sems = refs
    copies = [
        pltpu.make_async_copy(source, target, sems.at[place])
        for place, (source, target) in enumerate(
            [
                (index_hbm, index_ref),
                (frac_hbm, frac_ref),
                (start_hbm, start_ref),
                (aperture_hbm, aperture_ref),
                (traces_hbm, traces_ref),
            ]
        )
    ]
    for copy in copies:
        copy.start()
    for copy in copies[:4]:
        copy.wait()
    me = lax.axis_index("tile")
    rows = index_ref[...].astype(jnp.float32)
    weights = frac_ref[...].astype(jnp.float32)
    starts = start_ref[...]
    slots = aperture_ref[...]
    position = lax.broadcasted_iota(jnp.int32, rows.shape, 0)
    start_tile = lax.broadcasted_iota(jnp.int32, starts.shape, 0)
    start_block = lax.broadcasted_iota(jnp.int32, starts.shape, 1)
    slot_tile = lax.broadcasted_iota(jnp.int32, slots.shape, 1)
    for step, out_ref in enumerate(out_refs):
        tile, block = chip_of(step, tiles)
        for other in range(2):
            mine = position == (block ^ other)
            out_ref[other : other + 1] = jnp.sum(
                jnp.where(mine, rows, 0.0), axis=0, keepdims=True
            )
            out_ref[2 + other : 3 + other] = jnp.sum(
                jnp.where(mine, weights, 0.0), axis=0, keepdims=True
            )
            here = jnp.logical_and(start_tile == tile, start_block == (me ^ other))
            first = jnp.where(here, starts, 0).astype(jnp.float32)
            first = jnp.sum(jnp.sum(first, axis=1, keepdims=True), axis=0, keepdims=True)
            hits = jnp.logical_and(slot_tile == tile, slots == (me ^ other))
            hits = jnp.where(hits, 1.0, 0.0)
            hits = jnp.max(jnp.max(hits, axis=1, keepdims=True), axis=0, keepdims=True)
            code = jnp.where(hits > 0.0, first, -1.0).astype(jnp.int32)
            place = 2 * step + other
            codes_ref[place : place + 1] = jnp.broadcast_to(code, (1, codes_ref.shape[1]))
    copies[4].wait()


def interpolate(columns, other, shift, window):
    row = columns[:, other : other + 1] + shift
    weight = columns[:, 2 + other : 3 + other]
    depth = row.shape[0]
    lane = lax.broadcasted_iota(jnp.int32, (depth, window.shape[1]), 1).astype(jnp.float32)
    hot = jnp.concatenate(
        [(lane == row).astype(jnp.bfloat16), (lane == row + 1.0).astype(jnp.bfloat16)], axis=0
    )
    both = lax.dot_general(hot, window, NT_DIMS, preferred_element_type=jnp.float32)
    return ((1.0 - weight) * both[:depth] + weight * both[depth:]).astype(jnp.bfloat16)


def depth_kernel(step, codes_ref, own_ref, other_ref, wanted_ref, out_ref):
    last = own_ref.shape[2] // LANES - SLAB // LANES
    columns = wanted_ref[...].T
    for other, traces_ref in enumerate((own_ref, other_ref)):
        first = codes_ref[2 * step + other, 0]

        @pl.when(first >= 0)
        def _():
            slab = pl.multiple_of(jnp.minimum(first // LANES, last) * LANES, LANES)
            window = jnp.concatenate(
                [traces_ref[0, :, pl.ds(slab, SLAB)], traces_ref[1, :, pl.ds(slab, SLAB)]], axis=0
            )
            shift = (first - slab).astype(jnp.float32)
            out_ref[other] = interpolate(columns, other, shift, window)

        @pl.when(first < 0)
        def _():
            out_ref[other] = jnp.zeros(out_ref.shape[1:], out_ref.dtype)


def add_chips(tiles, steps, amplitude_ref, depth_refs, total_ref, fresh):
    receivers = amplitude_ref.shape[2]
    group = 4
    for base in range(0, len(steps), group):
        places = range(base, min(base + group, len(steps)))
        weights = []
        for place in places:
            _, block = chip_of(steps[place], tiles)
            weights += [amplitude_ref[block], amplitude_ref[block ^ 1]]
        weights = jnp.concatenate(weights, axis=1)
        for part in range(2):
            lanes = slice(part * receivers, (part + 1) * receivers)
            traces = jnp.concatenate(
                [depth_refs[place][other, :, lanes] for place in places for other in range(2)],
                axis=1,
            )
            added = lax.dot_general(traces, weights, NT_DIMS, preferred_element_type=jnp.float32)
            if base or not fresh:
                added = added + total_ref[part]
            total_ref[part] = added


def gather_kernel(tiles, steps, amplitude_ref, *refs):
    add_chips(tiles, steps, amplitude_ref, refs[:-1], refs[-1], True)


def partial_kernel(tiles, shots, steps, amplitude_ref, before_ref, *refs):
    my_shot = lax.axis_index("shot")
    depth_refs = refs[: len(steps)]
    own_ref, out_refs, total_ref = refs[len(steps)], refs[len(steps) + 1 : -1], refs[-1]
    span = own_ref.shape[1]
    total_ref[...] = before_ref[...]
    add_chips(tiles, steps, amplitude_ref, depth_refs, total_ref, False)
    for part in range(2):
        own_ref[part] = total_ref[part, pl.ds(pl.multiple_of(my_shot * span, span), span), :]
        for place, step in enumerate(steps_of(shots)):
            target = target_of(my_shot, step, shots)
            rows = pl.ds(pl.multiple_of(target * span, span), span)
            out_refs[place][part] = total_ref[part, rows, :].astype(jnp.bfloat16)


def add_shots(refs, sums):
    stack, first, second = sums
    for ref in refs:
        real = ref[0].astype(jnp.float32)
        imag = ref[1].astype(jnp.float32)
        inverse = 1.0 / jnp.maximum(jnp.sqrt(real * real + imag * imag), 1.0)
        stack, first, second = stack + real, first + real * inverse, second + imag * inverse
    return stack, first, second


def early_kernel(*refs):
    zero = jnp.zeros(refs[0].shape[1:], jnp.float32)
    sums = add_shots(refs[:-1], (zero, zero, zero))
    for place, value in enumerate(sums):
        refs[-1][place] = value


def image_kernel(shots, sums_ref, *refs):
    stack, first, second = add_shots(refs[:-1], (sums_ref[0], sums_ref[1], sums_ref[2]))
    refs[-1][...] = stack * (first * first + second * second) / (shots * shots)


def local(traces, start, depth_index, depth_frac, aperture, amplitude):
    tiles = lax.axis_size("tile")
    shots = lax.axis_size("shot")
    parts, _, receivers, samples = traces.shape
    depth = depth_index.shape[3]
    columns = amplitude.shape[3]
    piece = depth // shots
    chips = tiles // 2
    away = near_first(chips)
    params = pltpu.CompilerParams(vmem_limit_bytes=32 << 20)
    small = pltpu.CompilerParams(vmem_limit_bytes=8 << 20)

    other_traces = lax.ppermute(traces[:, 0], "tile", [(pos, pos ^ 1) for pos in range(tiles)])

    inputs = [depth_index[0, 0], depth_frac[0, 0], start[0], aperture[0].T, traces[:, 0]]
    own_traces, codes, *wanted = pl.pallas_call(
        functools.partial(wanted_kernel, tiles),
        out_shape=[
            jax.ShapeDtypeStruct((parts, receivers, samples), traces.dtype),
            jax.ShapeDtypeStruct((tiles, LANES), jnp.int32),
        ]
        + [jax.ShapeDtypeStruct((4, depth), jnp.float32)] * chips,
        in_specs=[HBM] * len(inputs),
        out_specs=[VMEM] * (2 + chips),
        scratch_shapes=[pltpu.VMEM(value.shape, value.dtype) for value in inputs[:-1]]
        + [pltpu.SemaphoreType.DMA((len(inputs),))],
        compiler_params=params,
    )(*[pltpu.with_memory_space_constraint(value, pltpu.HBM) for value in inputs])
    asked = {
        step: lax.ppermute(wanted[step], "tile", chip_pairs(step, tiles))
        for step in away
    }

    def depth_traces(step, request):
        return pl.pallas_call(
            functools.partial(depth_kernel, step),
            out_shape=jax.ShapeDtypeStruct((2, depth, parts * receivers), jnp.bfloat16),
            in_specs=[VMEM] * 4,
            out_specs=VMEM,
            compiler_params=params,
            cost_estimate=pl.CostEstimate(
                flops=8 * depth * SLAB * parts * receivers,
                bytes_accessed=8 * parts * receivers * (samples + depth),
                transcendentals=0,
            ),
        )(codes, own_traces, other_traces, request)

    kept = depth_traces(0, wanted[0])
    received = [kept]
    for step in away:
        request = asked[step]
        sent = depth_traces(step, request)
        received.append(lax.ppermute(sent, "tile", chip_pairs(step, tiles)))

    own = jax.ShapeDtypeStruct((parts, piece, columns), jnp.float32)
    other = jax.ShapeDtypeStruct((parts, piece, columns), jnp.bfloat16)
    steps = [0] + away
    total = jax.ShapeDtypeStruct((parts, depth, columns), jnp.float32)
    before = pl.pallas_call(
        functools.partial(gather_kernel, tiles, steps[:-1]),
        out_shape=total,
        in_specs=[VMEM] * chips,
        out_specs=VMEM,
        compiler_params=params,
    )(amplitude[0, 0], *received[:-1])
    pieces = pl.pallas_call(
        functools.partial(partial_kernel, tiles, shots, steps[-1:]),
        out_shape=[own] + [other] * (shots - 1),
        in_specs=[VMEM] * 3,
        out_specs=[VMEM] * shots,
        scratch_shapes=[pltpu.VMEM(total.shape, total.dtype)],
        compiler_params=params,
    )(amplitude[0, 0], before, received[-1])
    summed = [pieces[0]]
    for place, step in enumerate(steps_of(shots)):
        summed.append(lax.ppermute(pieces[1 + place], "shot", pairs(step, shots)))

    early = 2
    sums = pl.pallas_call(
        early_kernel,
        out_shape=jax.ShapeDtypeStruct((3, piece, columns), jnp.float32),
        in_specs=[VMEM] * early,
        out_specs=VMEM,
        compiler_params=params,
    )(*summed[:early])
    image = pl.pallas_call(
        functools.partial(image_kernel, shots),
        out_shape=jax.ShapeDtypeStruct((piece, columns), jnp.float32),
        in_specs=[VMEM] * (1 + shots - early),
        out_specs=VMEM,
        compiler_params=small,
    )(sums, *summed[early:])
    return image.T


def solution(mesh):
    in_specs = (
        P(None, "shot", "tile", None),
        P("shot", None, None),
        P("shot", "tile", None, None),
        P("shot", "tile", None, None),
        P("shot", None, None),
        P("shot", "tile", None, None, None),
    )
    out_specs = P("tile", "shot")
    return jax.shard_map(local, mesh=mesh, in_specs=in_specs, out_specs=out_specs, check_vma=False)
```

```python
import functools

import jax
import jax.numpy as jnp
from jax import lax
from jax.experimental import pallas as pl
from jax.experimental.pallas import tpu as pltpu
from jax.sharding import PartitionSpec as P

TW = 512
LANES = 128
SLAB = TW + LANES
NT_DIMS = (((1,), (1,)), ((), ()))
VMEM = pl.BlockSpec(memory_space=pltpu.VMEM)
HBM = pl.BlockSpec(memory_space=pltpu.HBM)


def target_of(pos, step, count):
    if count & (count - 1) == 0:
        return pos ^ step
    return (pos + step) % count


def source_of(pos, step, count):
    if count & (count - 1) == 0:
        return pos ^ step
    return (pos - step + count) % count


def pairs(step, count):
    return [(pos, target_of(pos, step, count)) for pos in range(count)]


def chip_pairs(step, tiles):
    return [
        (pos, 2 * target_of(pos // 2, step, tiles // 2) + pos % 2) for pos in range(tiles)
    ]


def steps_of(count):
    return list(range(count // 2, count)) + list(range(1, count // 2))


def near_first(count):
    return sorted(range(1, count), key=lambda step: (step.bit_count(), step))


def chip_of(step, tiles):
    me = lax.axis_index("tile")
    if step == 0:
        return me, me
    chips = tiles // 2
    served = 2 * target_of(me // 2, step, chips) + me % 2
    return served, 2 * source_of(me // 2, step, chips) + me % 2


def wanted_kernel(tiles, index_hbm, frac_hbm, start_hbm, aperture_hbm, traces_hbm, *refs):
    traces_ref, codes_ref, *out_refs, index_ref, frac_ref, start_ref, aperture_ref, sems = refs
    copies = [
        pltpu.make_async_copy(source, target, sems.at[place])
        for place, (source, target) in enumerate(
            [
                (index_hbm, index_ref),
                (frac_hbm, frac_ref),
                (start_hbm, start_ref),
                (aperture_hbm, aperture_ref),
                (traces_hbm, traces_ref),
            ]
        )
    ]
    for copy in copies:
        copy.start()
    for copy in copies[:4]:
        copy.wait()
    me = lax.axis_index("tile")
    rows = index_ref[...].astype(jnp.float32)
    weights = frac_ref[...].astype(jnp.float32)
    starts = start_ref[...]
    slots = aperture_ref[...]
    position = lax.broadcasted_iota(jnp.int32, rows.shape, 0)
    start_tile = lax.broadcasted_iota(jnp.int32, starts.shape, 0)
    start_block = lax.broadcasted_iota(jnp.int32, starts.shape, 1)
    slot_tile = lax.broadcasted_iota(jnp.int32, slots.shape, 1)
    for step, out_ref in enumerate(out_refs):
        tile, block = chip_of(step, tiles)
        for other in range(2):
            mine = position == (block ^ other)
            out_ref[other : other + 1] = jnp.sum(
                jnp.where(mine, rows, 0.0), axis=0, keepdims=True
            )
            out_ref[2 + other : 3 + other] = jnp.sum(
                jnp.where(mine, weights, 0.0), axis=0, keepdims=True
            )
            here = jnp.logical_and(start_tile == tile, start_block == (me ^ other))
            first = jnp.where(here, starts, 0).astype(jnp.float32)
            first = jnp.sum(jnp.sum(first, axis=1, keepdims=True), axis=0, keepdims=True)
            hits = jnp.logical_and(slot_tile == tile, slots == (me ^ other))
            hits = jnp.where(hits, 1.0, 0.0)
            hits = jnp.max(jnp.max(hits, axis=1, keepdims=True), axis=0, keepdims=True)
            code = jnp.where(hits > 0.0, first, -1.0).astype(jnp.int32)
            place = 2 * step + other
            codes_ref[place : place + 1] = jnp.broadcast_to(code, (1, codes_ref.shape[1]))
    copies[4].wait()


def interpolate(columns, other, shift, window):
    row = columns[:, other : other + 1] + shift
    weight = columns[:, 2 + other : 3 + other]
    depth = row.shape[0]
    lane = lax.broadcasted_iota(jnp.int32, (depth, window.shape[1]), 1).astype(jnp.float32)
    hot = jnp.concatenate(
        [(lane == row).astype(jnp.bfloat16), (lane == row + 1.0).astype(jnp.bfloat16)], axis=0
    )
    both = lax.dot_general(hot, window, NT_DIMS, preferred_element_type=jnp.float32)
    return ((1.0 - weight) * both[:depth] + weight * both[depth:]).astype(jnp.bfloat16)


def depth_kernel(step, codes_ref, own_ref, other_ref, wanted_ref, out_ref):
    last = own_ref.shape[2] // LANES - SLAB // LANES
    columns = wanted_ref[...].T
    for other, traces_ref in enumerate((own_ref, other_ref)):
        first = codes_ref[2 * step + other, 0]

        @pl.when(first >= 0)
        def _():
            slab = pl.multiple_of(jnp.minimum(first // LANES, last) * LANES, LANES)
            window = jnp.concatenate(
                [traces_ref[0, :, pl.ds(slab, SLAB)], traces_ref[1, :, pl.ds(slab, SLAB)]], axis=0
            )
            shift = (first - slab).astype(jnp.float32)
            out_ref[other] = interpolate(columns, other, shift, window)

        @pl.when(first < 0)
        def _():
            out_ref[other] = jnp.zeros(out_ref.shape[1:], out_ref.dtype)


def add_chips(tiles, steps, amplitude_ref, depth_refs, total_ref, fresh):
    receivers = amplitude_ref.shape[2]
    group = 4
    for base in range(0, len(steps), group):
        places = range(base, min(base + group, len(steps)))
        weights = []
        for place in places:
            _, block = chip_of(steps[place], tiles)
            weights += [amplitude_ref[block], amplitude_ref[block ^ 1]]
        weights = jnp.concatenate(weights, axis=1)
        for part in range(2):
            lanes = slice(part * receivers, (part + 1) * receivers)
            traces = jnp.concatenate(
                [depth_refs[place][other, :, lanes] for place in places for other in range(2)],
                axis=1,
            )
            added = lax.dot_general(traces, weights, NT_DIMS, preferred_element_type=jnp.float32)
            if base or not fresh:
                added = added + total_ref[part]
            total_ref[part] = added


def gather_kernel(tiles, steps, amplitude_ref, *refs):
    add_chips(tiles, steps, amplitude_ref, refs[:-1], refs[-1], True)


def partial_kernel(tiles, shots, steps, amplitude_ref, before_ref, *refs):
    my_shot = lax.axis_index("shot")
    depth_refs = refs[: len(steps)]
    own_ref, out_refs, total_ref = refs[len(steps)], refs[len(steps) + 1 : -1], refs[-1]
    span = own_ref.shape[1]
    total_ref[...] = before_ref[...]
    add_chips(tiles, steps, amplitude_ref, depth_refs, total_ref, False)
    for part in range(2):
        own_ref[part] = total_ref[part, pl.ds(pl.multiple_of(my_shot * span, span), span), :]
        for place, step in enumerate(steps_of(shots)):
            target = target_of(my_shot, step, shots)
            rows = pl.ds(pl.multiple_of(target * span, span), span)
            out_refs[place][part] = total_ref[part, rows, :].astype(jnp.bfloat16)


def add_shots(refs, sums):
    stack, first, second = sums
    for ref in refs:
        real = ref[0].astype(jnp.float32)
        imag = ref[1].astype(jnp.float32)
        inverse = 1.0 / jnp.maximum(jnp.sqrt(real * real + imag * imag), 1.0)
        stack, first, second = stack + real, first + real * inverse, second + imag * inverse
    return stack, first, second


def early_kernel(*refs):
    zero = jnp.zeros(refs[0].shape[1:], jnp.float32)
    sums = add_shots(refs[:-1], (zero, zero, zero))
    for place, value in enumerate(sums):
        refs[-1][place] = value


def image_kernel(shots, sums_ref, *refs):
    stack, first, second = add_shots(refs[:-1], (sums_ref[0], sums_ref[1], sums_ref[2]))
    refs[-1][...] = stack * (first * first + second * second) / (shots * shots)


def local(traces, start, depth_index, depth_frac, aperture, amplitude):
    tiles = lax.axis_size("tile")
    shots = lax.axis_size("shot")
    parts, _, receivers, samples = traces.shape
    depth = depth_index.shape[3]
    columns = amplitude.shape[3]
    piece = depth // shots
    chips = tiles // 2
    away = near_first(chips)
    params = pltpu.CompilerParams(vmem_limit_bytes=32 << 20)
    small = pltpu.CompilerParams(vmem_limit_bytes=8 << 20)

    other_traces = lax.ppermute(traces[:, 0], "tile", [(pos, pos ^ 1) for pos in range(tiles)])

    inputs = [depth_index[0, 0], depth_frac[0, 0], start[0], aperture[0].T, traces[:, 0]]
    own_traces, codes, *wanted = pl.pallas_call(
        functools.partial(wanted_kernel, tiles),
        out_shape=[
            jax.ShapeDtypeStruct((parts, receivers, samples), traces.dtype),
            jax.ShapeDtypeStruct((tiles, LANES), jnp.int32),
        ]
        + [jax.ShapeDtypeStruct((4, depth), jnp.float32)] * chips,
        in_specs=[HBM] * len(inputs),
        out_specs=[VMEM] * (2 + chips),
        scratch_shapes=[pltpu.VMEM(value.shape, value.dtype) for value in inputs[:-1]]
        + [pltpu.SemaphoreType.DMA((len(inputs),))],
        compiler_params=params,
    )(*[pltpu.with_memory_space_constraint(value, pltpu.HBM) for value in inputs])
    asked = {
        step: lax.ppermute(wanted[step], "tile", chip_pairs(step, tiles))
        for step in away
    }

    def depth_traces(step, request):
        return pl.pallas_call(
            functools.partial(depth_kernel, step),
            out_shape=jax.ShapeDtypeStruct((2, depth, parts * receivers), jnp.bfloat16),
            in_specs=[VMEM] * 4,
            out_specs=VMEM,
            compiler_params=params,
            cost_estimate=pl.CostEstimate(
                flops=8 * depth * SLAB * parts * receivers,
                bytes_accessed=8 * parts * receivers * (samples + depth),
                transcendentals=0,
            ),
        )(codes, own_traces, other_traces, request)

    kept = depth_traces(0, wanted[0])
    received = [kept]
    for step in away:
        request = asked[step]
        sent = depth_traces(step, request)
        received.append(lax.ppermute(sent, "tile", chip_pairs(step, tiles)))

    own = jax.ShapeDtypeStruct((parts, piece, columns), jnp.float32)
    other = jax.ShapeDtypeStruct((parts, piece, columns), jnp.bfloat16)
    steps = [0] + away
    early = (chips + 1) // 2
    total = jax.ShapeDtypeStruct((parts, depth, columns), jnp.float32)
    before = pl.pallas_call(
        functools.partial(gather_kernel, tiles, steps[:early]),
        out_shape=total,
        in_specs=[VMEM] * (1 + early),
        out_specs=VMEM,
        compiler_params=params,
    )(amplitude[0, 0], *received[:early])
    pieces = pl.pallas_call(
        functools.partial(partial_kernel, tiles, shots, steps[early:]),
        out_shape=[own] + [other] * (shots - 1),
        in_specs=[VMEM] * (2 + chips - early),
        out_specs=[VMEM] * shots,
        scratch_shapes=[pltpu.VMEM(total.shape, total.dtype)],
        compiler_params=params,
    )(amplitude[0, 0], before, *received[early:])
    summed = [pieces[0]]
    for place, step in enumerate(steps_of(shots)):
        summed.append(lax.ppermute(pieces[1 + place], "shot", pairs(step, shots)))

    early = 2
    sums = pl.pallas_call(
        early_kernel,
        out_shape=jax.ShapeDtypeStruct((3, piece, columns), jnp.float32),
        in_specs=[VMEM] * early,
        out_specs=VMEM,
        compiler_params=params,
    )(*summed[:early])
    image = pl.pallas_call(
        functools.partial(image_kernel, shots),
        out_shape=jax.ShapeDtypeStruct((piece, columns), jnp.float32),
        in_specs=[VMEM] * (1 + shots - early),
        out_specs=VMEM,
        compiler_params=small,
    )(sums, *summed[early:])
    return image.T


def solution(mesh):
    in_specs = (
        P(None, "shot", "tile", None),
        P("shot", None, None),
        P("shot", "tile", None, None),
        P("shot", "tile", None, None),
        P("shot", None, None),
        P("shot", "tile", None, None, None),
    )
    out_specs = P("tile", "shot")
    return jax.shard_map(local, mesh=mesh, in_specs=in_specs, out_specs=out_specs, check_vma=False)
```

```python
import functools

import jax
import jax.numpy as jnp
from jax import lax
from jax.experimental import pallas as pl
from jax.experimental.pallas import tpu as pltpu
from jax.sharding import PartitionSpec as P

TW = 512
LANES = 128
SLAB = TW + LANES
NT_DIMS = (((1,), (1,)), ((), ()))
VMEM = pl.BlockSpec(memory_space=pltpu.VMEM)
HBM = pl.BlockSpec(memory_space=pltpu.HBM)


def target_of(pos, step, count):
    if count & (count - 1) == 0:
        return pos ^ step
    return (pos + step) % count


def source_of(pos, step, count):
    if count & (count - 1) == 0:
        return pos ^ step
    return (pos - step + count) % count


def pairs(step, count):
    return [(pos, target_of(pos, step, count)) for pos in range(count)]


def chip_pairs(step, tiles):
    return [
        (pos, 2 * target_of(pos // 2, step, tiles // 2) + pos % 2) for pos in range(tiles)
    ]


def steps_of(count):
    return list(range(count // 2, count)) + list(range(1, count // 2))


def near_first(count):
    return sorted(range(1, count), key=lambda step: (step.bit_count(), step))


def chip_of(step, tiles):
    me = lax.axis_index("tile")
    if step == 0:
        return me, me
    chips = tiles // 2
    served = 2 * target_of(me // 2, step, chips) + me % 2
    return served, 2 * source_of(me // 2, step, chips) + me % 2


def wanted_kernel(tiles, index_hbm, frac_hbm, start_hbm, aperture_hbm, traces_hbm, *refs):
    traces_ref, codes_ref, *out_refs, index_ref, frac_ref, start_ref, aperture_ref, sems = refs
    copies = [
        pltpu.make_async_copy(source, target, sems.at[place])
        for place, (source, target) in enumerate(
            [
                (index_hbm, index_ref),
                (frac_hbm, frac_ref),
                (start_hbm, start_ref),
                (aperture_hbm, aperture_ref),
                (traces_hbm, traces_ref),
            ]
        )
    ]
    for copy in copies:
        copy.start()
    for copy in copies[:4]:
        copy.wait()
    me = lax.axis_index("tile")
    rows = index_ref[...].astype(jnp.float32)
    weights = frac_ref[...].astype(jnp.float32)
    starts = start_ref[...]
    slots = aperture_ref[...]
    position = lax.broadcasted_iota(jnp.int32, rows.shape, 0)
    start_tile = lax.broadcasted_iota(jnp.int32, starts.shape, 0)
    start_block = lax.broadcasted_iota(jnp.int32, starts.shape, 1)
    slot_tile = lax.broadcasted_iota(jnp.int32, slots.shape, 1)
    for step, out_ref in enumerate(out_refs):
        tile, block = chip_of(step, tiles)
        for other in range(2):
            mine = position == (block ^ other)
            out_ref[other : other + 1] = jnp.sum(
                jnp.where(mine, rows, 0.0), axis=0, keepdims=True
            )
            out_ref[2 + other : 3 + other] = jnp.sum(
                jnp.where(mine, weights, 0.0), axis=0, keepdims=True
            )
            here = jnp.logical_and(start_tile == tile, start_block == (me ^ other))
            first = jnp.where(here, starts, 0).astype(jnp.float32)
            first = jnp.sum(jnp.sum(first, axis=1, keepdims=True), axis=0, keepdims=True)
            hits = jnp.logical_and(slot_tile == tile, slots == (me ^ other))
            hits = jnp.where(hits, 1.0, 0.0)
            hits = jnp.max(jnp.max(hits, axis=1, keepdims=True), axis=0, keepdims=True)
            code = jnp.where(hits > 0.0, first, -1.0).astype(jnp.int32)
            place = 2 * step + other
            codes_ref[place : place + 1] = jnp.broadcast_to(code, (1, codes_ref.shape[1]))
    copies[4].wait()


def interpolate(columns, other, shift, window):
    row = columns[:, other : other + 1] + shift
    weight = columns[:, 2 + other : 3 + other]
    depth = row.shape[0]
    lane = lax.broadcasted_iota(jnp.int32, (depth, window.shape[1]), 1).astype(jnp.float32)
    hot = jnp.concatenate(
        [(lane == row).astype(jnp.bfloat16), (lane == row + 1.0).astype(jnp.bfloat16)], axis=0
    )
    both = lax.dot_general(hot, window, NT_DIMS, preferred_element_type=jnp.float32)
    return ((1.0 - weight) * both[:depth] + weight * both[depth:]).astype(jnp.bfloat16)


def depth_kernel(step, codes_ref, own_ref, other_ref, wanted_ref, out_ref):
    last = own_ref.shape[2] // LANES - SLAB // LANES
    columns = wanted_ref[...].T
    for other, traces_ref in enumerate((own_ref, other_ref)):
        first = codes_ref[2 * step + other, 0]

        @pl.when(first >= 0)
        def _():
            slab = pl.multiple_of(jnp.minimum(first // LANES, last) * LANES, LANES)
            window = jnp.concatenate(
                [traces_ref[0, :, pl.ds(slab, SLAB)], traces_ref[1, :, pl.ds(slab, SLAB)]], axis=0
            )
            shift = (first - slab).astype(jnp.float32)
            out_ref[other] = interpolate(columns, other, shift, window)

        @pl.when(first < 0)
        def _():
            out_ref[other] = jnp.zeros(out_ref.shape[1:], out_ref.dtype)


def add_chips(tiles, steps, amplitude_ref, depth_refs, total_ref, before_ref):
    receivers = amplitude_ref.shape[2]
    group = 4
    for base in range(0, len(steps), group):
        places = range(base, min(base + group, len(steps)))
        weights = []
        for place in places:
            _, block = chip_of(steps[place], tiles)
            weights += [amplitude_ref[block], amplitude_ref[block ^ 1]]
        weights = jnp.concatenate(weights, axis=1)
        for part in range(2):
            lanes = slice(part * receivers, (part + 1) * receivers)
            traces = jnp.concatenate(
                [depth_refs[place][other, :, lanes] for place in places for other in range(2)],
                axis=1,
            )
            added = lax.dot_general(traces, weights, NT_DIMS, preferred_element_type=jnp.float32)
            if base:
                added = added + total_ref[part]
            elif before_ref is not None:
                added = added + before_ref[part]
            total_ref[part] = added


def gather_kernel(tiles, steps, amplitude_ref, *refs):
    add_chips(tiles, steps, amplitude_ref, refs[:-1], refs[-1], None)


def partial_kernel(tiles, shots, steps, amplitude_ref, before_ref, *refs):
    my_shot = lax.axis_index("shot")
    depth_refs = refs[: len(steps)]
    own_ref, out_refs, total_ref = refs[len(steps)], refs[len(steps) + 1 : -1], refs[-1]
    span = own_ref.shape[1]
    add_chips(tiles, steps, amplitude_ref, depth_refs, total_ref, before_ref)
    for part in range(2):
        own_ref[part] = total_ref[part, pl.ds(pl.multiple_of(my_shot * span, span), span), :]
        for place, step in enumerate(steps_of(shots)):
            target = target_of(my_shot, step, shots)
            rows = pl.ds(pl.multiple_of(target * span, span), span)
            out_refs[place][part] = total_ref[part, rows, :].astype(jnp.bfloat16)


def add_shots(refs, sums):
    stack, first, second = sums
    for ref in refs:
        real = ref[0].astype(jnp.float32)
        imag = ref[1].astype(jnp.float32)
        inverse = 1.0 / jnp.maximum(jnp.sqrt(real * real + imag * imag), 1.0)
        stack, first, second = stack + real, first + real * inverse, second + imag * inverse
    return stack, first, second


def early_kernel(*refs):
    zero = jnp.zeros(refs[0].shape[1:], jnp.float32)
    sums = add_shots(refs[:-1], (zero, zero, zero))
    for place, value in enumerate(sums):
        refs[-1][place] = value


def image_kernel(shots, sums_ref, *refs):
    stack, first, second = add_shots(refs[:-1], (sums_ref[0], sums_ref[1], sums_ref[2]))
    refs[-1][...] = stack * (first * first + second * second) / (shots * shots)


def local(traces, start, depth_index, depth_frac, aperture, amplitude):
    tiles = lax.axis_size("tile")
    shots = lax.axis_size("shot")
    parts, _, receivers, samples = traces.shape
    depth = depth_index.shape[3]
    columns = amplitude.shape[3]
    piece = depth // shots
    chips = tiles // 2
    away = near_first(chips)
    params = pltpu.CompilerParams(vmem_limit_bytes=32 << 20)
    small = pltpu.CompilerParams(vmem_limit_bytes=8 << 20)

    other_traces = lax.ppermute(traces[:, 0], "tile", [(pos, pos ^ 1) for pos in range(tiles)])

    inputs = [depth_index[0, 0], depth_frac[0, 0], start[0], aperture[0].T, traces[:, 0]]
    own_traces, codes, *wanted = pl.pallas_call(
        functools.partial(wanted_kernel, tiles),
        out_shape=[
            jax.ShapeDtypeStruct((parts, receivers, samples), traces.dtype),
            jax.ShapeDtypeStruct((tiles, LANES), jnp.int32),
        ]
        + [jax.ShapeDtypeStruct((4, depth), jnp.float32)] * chips,
        in_specs=[HBM] * len(inputs),
        out_specs=[VMEM] * (2 + chips),
        scratch_shapes=[pltpu.VMEM(value.shape, value.dtype) for value in inputs[:-1]]
        + [pltpu.SemaphoreType.DMA((len(inputs),))],
        compiler_params=params,
    )(*[pltpu.with_memory_space_constraint(value, pltpu.HBM) for value in inputs])
    asked = {
        step: lax.ppermute(wanted[step], "tile", chip_pairs(step, tiles))
        for step in away
    }

    def depth_traces(step, request):
        return pl.pallas_call(
            functools.partial(depth_kernel, step),
            out_shape=jax.ShapeDtypeStruct((2, depth, parts * receivers), jnp.bfloat16),
            in_specs=[VMEM] * 4,
            out_specs=VMEM,
            compiler_params=params,
            cost_estimate=pl.CostEstimate(
                flops=8 * depth * SLAB * parts * receivers,
                bytes_accessed=8 * parts * receivers * (samples + depth),
                transcendentals=0,
            ),
        )(codes, own_traces, other_traces, request)

    kept = depth_traces(0, wanted[0])
    received = [kept]
    for step in away:
        request = asked[step]
        sent = depth_traces(step, request)
        received.append(lax.ppermute(sent, "tile", chip_pairs(step, tiles)))

    own = jax.ShapeDtypeStruct((parts, piece, columns), jnp.float32)
    other = jax.ShapeDtypeStruct((parts, piece, columns), jnp.bfloat16)
    steps = [0] + away
    early = (chips + 1) // 2
    total = jax.ShapeDtypeStruct((parts, depth, columns), jnp.float32)
    before = pl.pallas_call(
        functools.partial(gather_kernel, tiles, steps[:early]),
        out_shape=total,
        in_specs=[VMEM] * (1 + early),
        out_specs=VMEM,
        compiler_params=params,
    )(amplitude[0, 0], *received[:early])
    pieces = pl.pallas_call(
        functools.partial(partial_kernel, tiles, shots, steps[early:]),
        out_shape=[own] + [other] * (shots - 1),
        in_specs=[VMEM] * (2 + chips - early),
        out_specs=[VMEM] * shots,
        scratch_shapes=[pltpu.VMEM(total.shape, total.dtype)],
        compiler_params=params,
    )(amplitude[0, 0], before, *received[early:])
    summed = [pieces[0]]
    for place, step in enumerate(steps_of(shots)):
        summed.append(lax.ppermute(pieces[1 + place], "shot", pairs(step, shots)))

    early = 2
    sums = pl.pallas_call(
        early_kernel,
        out_shape=jax.ShapeDtypeStruct((3, piece, columns), jnp.float32),
        in_specs=[VMEM] * early,
        out_specs=VMEM,
        compiler_params=params,
    )(*summed[:early])
    image = pl.pallas_call(
        functools.partial(image_kernel, shots),
        out_shape=jax.ShapeDtypeStruct((piece, columns), jnp.float32),
        in_specs=[VMEM] * (1 + shots - early),
        out_specs=VMEM,
        compiler_params=small,
    )(sums, *summed[early:])
    return image.T


def solution(mesh):
    in_specs = (
        P(None, "shot", "tile", None),
        P("shot", None, None),
        P("shot", "tile", None, None),
        P("shot", "tile", None, None),
        P("shot", None, None),
        P("shot", "tile", None, None, None),
    )
    out_specs = P("tile", "shot")
    return jax.shard_map(local, mesh=mesh, in_specs=in_specs, out_specs=out_specs, check_vma=False)
```
